32 devices in a mesh: occ: 4 (over x, core), vir: 8 (over z, y).
Axes of the slice: x: 2, y: 2, z: 4, core: 2. Of those that a mesh axis runs over, the one named last changes fastest.
Arguments:
- amps: bfloat16 [4096, 3072], P('occ', 'vir'), may hold values from -6 to 6
- ints: bfloat16 [3072, 4096], P(None, 'vir'), may hold values from -0.109375 to 0.109375
- amp_mask: int32 [128, 6], P('occ'), may hold values 0 or 1
- keep_mask: int32 [128, 8], P('occ', 'vir'), may hold values 0 or 1
- owners: int32 [128, 1], P('occ'), may hold values from 0 to 3; in each aligned block of 32 rows (0 to 31, 32 to 63, ...) at most 16 rows name the same one
- occ_energy: bfloat16 [4096], P('occ'), may hold values from -2 to -0.5
- vir_energy: float32 [4096], P('vir'), may hold values from 0.5 to 3
- mix: bfloat16 [4, 32, 32], P('occ'), may hold values from -4 to 4
Outputs:
- owned: bfloat16 [256, 32, 4096], P('occ', None, 'vir')
The draws below stay inside these ranges and needn't reach their ends.
Inputs may be any that keep to these rules, and one draw needn't show every extreme that they name: `owners`: in the row tiles of one index of occ no owner appears more than 16 times; in every draw some owner appears exactly 16 times in some device's tiles.
All inputs are finite; a program needn't handle non-finite values. No bound on the sum of `amp_mask` or of `keep_mask` on one device may be relied on, other than what follows from the above.
Results may differ from the reference program's by a relative error of at most 0.0049.
Values may be sent and summed in bfloat16 or wider, within the bound.
A program may use at most 64 MiB of HBM per device.

```python
import math
import jax
import jax.numpy as jnp
import numpy as np

TILE = 512
KT = 6
RT = 32
TILES_DEV = 32
COL_DEV = 512
K = 3072
ROW_TILES = 128
ROWS = 4096
COLS = 4096
OWNERS = 4
CAP = 16
SLOTS = 256
N_VIR = 8


def draw_mix(key, part):
    noise = jax.random.normal(key, (OWNERS, RT, RT), jnp.float32)
    noise = jnp.clip(noise, -5.0, 5.0)
    return (jnp.eye(RT, dtype=jnp.float32)[None] + 0.6 * noise / math.sqrt(RT)).astype(jnp.bfloat16)


def set_ends(entries, own_key, least, largest):
    place = [jax.random.randint(jax.random.fold_in(own_key, axis), (), 0, length) for axis, length in enumerate(entries.shape)]
    widest = entries.shape.index(max(entries.shape))
    next_to = place[:widest] + [(place[widest] + 1) % entries.shape[widest]] + place[widest + 1:]
    return entries.at[tuple(place)].set(least).at[tuple(next_to)].set(largest)


def steps_of(rng, extent, pieces, least, top_value):
    def one(dim, blocks):
        draws = jax.random.uniform(jax.random.fold_in(jax.random.fold_in(rng, 6), dim), (blocks,), jnp.float32, least / len(pieces), top_value / len(pieces))
        return jnp.repeat(jnp.exp(draws), extent[dim] // blocks).reshape((-1,) + (1,) * (len(extent) - dim - 1))

    factor_of = one(*pieces[0])
    for cut in pieces[1:]:
        factor_of = factor_of * one(*cut)
    return factor_of


def routed_block(rng, own, number, rows, number_of, top, limit, slope):
    order = jax.random.permutation(rng, number_of)
    heavy_load, common = portions_of(number_of, rows * top, limit, slope, True), portions_of(number_of, rows * top, limit, slope, False)
    places = jnp.arange(number_of)

    def named(sizes, turn):
        used = int((sizes > 0).sum())
        fixed = max(1, used // 4)
        moved = fixed + (places - fixed + turn * (used - fixed)) % max(1, number_of - fixed)
        return jnp.zeros((number_of,), jnp.int32).at[order[jnp.where(places < fixed, places, moved)]].set(jnp.asarray(sizes, jnp.int32))

    sizes = jnp.where(number % 4 == 0, named(heavy_load, number // 4), named(common, number - number // 4 - 1))
    mixed = jax.random.permutation(jax.random.fold_in(own, 3), number_of)
    giver, receiver = mixed[0:number_of // 2 * 2:2], mixed[1:number_of // 2 * 2:2]
    margin = jnp.minimum(sizes[giver] - 1, limit - sizes[receiver]) // 2
    margin = jnp.where((giver == order[0]) | (receiver == order[0]) | (sizes[receiver] == 0), 0, jnp.maximum(margin, 0))
    moved = jax.random.randint(jax.random.fold_in(own, 4), (number_of // 2,), 0, 1 << 20) % (margin + 1)
    sizes = sizes.at[giver].add(-moved).at[receiver].add(moved)
    members = jnp.searchsorted(jnp.cumsum(sizes), jnp.arange(rows * top), side="right").astype(jnp.int32)
    table = members.reshape(top, rows).T
    table = table[jax.random.permutation(jax.random.fold_in(own, 1), rows)]
    turn = jax.random.randint(jax.random.fold_in(own, 2), (rows, 1), 0, top)
    return jnp.take_along_axis(table, (jnp.arange(top)[None, :] + turn) % top, axis=1)


def portions_of(amount, total, bound, slope, full):
    loads = [(1 << 20) // math.isqrt(grade ** slope) + 1 for grade in range(1, amount + 1)]
    largest = bound if full else min(bound, max(-(-total // amount), total * loads[0] // sum(loads)))
    least = 1 if total - largest >= amount - 1 else 0
    holding, rest = [largest] + [least] * (amount - 1), total - largest - least * (amount - 1)
    while rest > 0:
        movable = [i for i in range(1, amount) if holding[i] < largest] or [i for i in range(1, amount) if holding[i] < bound]
        whole, left = sum([loads[i] for i in movable]), rest
        for i in movable:
            extra = min(bound - holding[i], max(1, left * loads[i] // whole), rest)
            holding[i] = holding[i] + extra
            rest = rest - extra
    return np.array(holding)


def centred(own_key, extent, deviation, limit, shards=(), held_as=jnp.bfloat16):
    values = deviation * jax.random.normal(own_key, extent, jnp.float32)
    if shards:
        values = values * steps_of(own_key, extent, shards, -0.22, 0.18)
    return jnp.clip(values, -limit, limit).astype(held_as)


def setup_inputs(seed: int = 0) -> dict:
    keys = jax.random.split(jax.random.key(seed), 9)
    amps = centred(keys[0], (ROWS, K), 1.0, 6.0, ((0, 4), (1, 8)))
    ints = centred(keys[1], (K, COLS), K ** -0.5, 0.109375, ((1, 8),))
    amp_mask = set_ends((jax.random.randint(keys[2], (ROW_TILES, KT), 0, 3) < 2).astype(jnp.int32), jax.random.fold_in(keys[2], 1), 0, 1)
    keep_mask = set_ends((jax.random.randint(keys[3], (ROW_TILES, N_VIR), 0, 4) < 3).astype(jnp.int32), jax.random.fold_in(keys[3], 1), 0, 1)
    owners_keys = jax.random.split(jax.random.fold_in(keys[4], 1), ROW_TILES // TILES_DEV)
    owners_turns = jax.random.permutation(jax.random.fold_in(keys[4], 3), ROW_TILES // TILES_DEV)
    owners = jax.vmap(lambda own, number: routed_block(jax.random.fold_in(keys[4], 2), own, number, TILES_DEV, OWNERS, 1, CAP, 2))(owners_keys, owners_turns).reshape((ROW_TILES, 1))
    occ_energy = jnp.clip(-2.0 + 1.5 * jax.random.uniform(keys[5], (ROWS,), jnp.float32) ** steps_of(keys[5], (ROWS,), ((0, 4),), -0.2, 0.2), -2.0, -0.5).astype(jnp.bfloat16)
    vir_energy = jnp.clip(0.5 + 2.5 * jax.random.uniform(keys[6], (COLS,), jnp.float32) ** steps_of(keys[6], (COLS,), ((0, 8),), -0.2, 0.2), 0.5, 3.0)
    mix = draw_mix(jax.random.fold_in(keys[8], 71), 0)
    return {"amps": amps, "ints": ints, "amp_mask": amp_mask, "keep_mask": keep_mask, "owners": owners, "occ_energy": occ_energy, "vir_energy": vir_energy, "mix": mix}


def reference(amps, ints, amp_mask, keep_mask, owners, occ_energy, vir_energy, mix):
    k_tile = jnp.arange(K) // TILE
    amp_cols = amp_mask.astype(jnp.float32)[:, k_tile]
    amp_full = jnp.repeat(amp_cols, RT, axis=0)
    masked = (amps.astype(jnp.float32) * amp_full).astype(jnp.bfloat16)
    ladder = jnp.dot(masked, ints, preferred_element_type=jnp.float32).astype(jnp.bfloat16)
    keep_full = jnp.repeat(jnp.repeat(keep_mask.astype(jnp.float32), RT, axis=0), COL_DEV, axis=1)
    kept = (ladder.astype(jnp.float32) * keep_full).astype(jnp.bfloat16)
    tiles = kept.reshape(ROW_TILES, RT, COLS)
    destination = owners[:, 0]
    weights = mix[destination].astype(jnp.float32)
    mixed_rows = jnp.einsum("tij,tjc->tic", weights, tiles.astype(jnp.float32))
    denominator = vir_energy[None, None, :] - occ_energy.astype(jnp.float32).reshape(ROW_TILES, RT)[:, :, None]
    update = (mixed_rows / denominator).astype(jnp.bfloat16)
    grouped = destination.reshape(OWNERS, TILES_DEV)
    same_owner = grouped[:, :, None] == grouped[:, None, :]
    earlier = jnp.arange(TILES_DEV)[:, None] > jnp.arange(TILES_DEV)[None, :]
    position = jnp.sum((same_owner & earlier[None]).astype(jnp.int32), axis=2).reshape(-1)
    source = (jnp.arange(ROW_TILES) // TILES_DEV).astype(jnp.int32)
    slot_index = (destination * (OWNERS * CAP) + source * CAP + position).astype(jnp.int32)
    owned = jnp.zeros((SLOTS, RT, COLS), jnp.bfloat16).at[slot_index].set(update)
    return owned
```

```python
import functools

import jax
import jax.numpy as jnp
from jax import lax
from jax.experimental import pallas as pl
from jax.experimental.pallas import tpu as pltpu
from jax.sharding import PartitionSpec as P

MESH = pl.DeviceIdType.MESH


def ladder_kernel(
    cfg, amps, ints, amp_mask, keep, own_s, own_v, occ, vir, mix, out,
    gath, ints_v, tiles, mix_all, own_all, own_tab, nxt,
    lsem, rsem_g, ssem_g, rsem_t, ssem_c, ssem_t, rsem_o, ssem_o,
):
    no, nv, td, tr, chunk_tiles, ahead, k_tile = cfg
    ng, nz = no // 2, nv // 2
    rows, kw = amps.shape
    cols = ints.shape[1]
    cr = chunk_tiles * tr
    nc = rows // cr
    cap = out.shape[0] // no
    o, v = lax.axis_index("occ"), lax.axis_index("vir")
    g, c = o // 2, o % 2
    z, y = v // 2, v % 2
    partner = {"occ": g * 2 + (1 - c), "vir": v}
    side = {"occ": o, "vir": z * 2 + (1 - y)}
    above = {"occ": o, "vir": (z + 1) * 2 + y}
    below = {"occ": o, "vir": (z - 1) * 2 + y}

    local = [
        pltpu.make_async_copy(own_v, own_all.at[o], lsem.at[0]),
        pltpu.make_async_copy(mix.at[0], mix_all.at[o], lsem.at[1]),
        pltpu.make_async_copy(amps, gath.at[v], lsem.at[2]),
        pltpu.make_async_copy(ints, ints_v, lsem.at[3]),
    ]
    for copy in local:
        copy.start()

    barrier = pltpu.get_barrier_semaphore()

    def greet(device):
        pl.semaphore_signal(barrier, inc=1, device_id=device, device_id_type=MESH)

    for d in range(1, no):
        greet({"occ": (o + d) % no, "vir": v})
    greet(side)

    @pl.when(z < nz - 1)
    def _():
        greet(above)

    @pl.when(z > 0)
    def _():
        greet(below)

    inner = jnp.where(z < nz - 1, 1, 0) + jnp.where(z > 0, 1, 0)
    pl.semaphore_wait(barrier, no + inner)

    def piece(src, slot, i, send_sem, device):
        window = pl.ds(pl.multiple_of(i * cr, cr), cr)
        return pltpu.make_async_remote_copy(
            src_ref=src.at[window], dst_ref=gath.at[slot, window], send_sem=send_sem,
            recv_sem=rsem_g.at[slot, i], device_id=device, device_id_type=MESH,
        )

    def spread(src, slot, i, up, down):
        zz = slot // 2
        if up:
            @pl.when(z < nz - 1)
            def _():
                piece(src, slot, i, ssem_g.at[0, zz], above).start()
        if down:
            @pl.when(z > 0)
            def _():
                piece(src, slot, i, ssem_g.at[1, zz], below).start()
        piece(src, slot, i, ssem_g.at[2, zz], side).start()

    def arrive(slot, i):
        piece(gath.at[slot], slot, i, ssem_g.at[2, 0], side).wait_recv()

    for i in range(min(ahead, nc)):
        spread(amps, v, i, True, True)

    def small(d, o2):
        peer = {"occ": (o + d) % no, "vir": v}
        return [
            pltpu.make_async_remote_copy(
                src_ref=own_v, dst_ref=own_all.at[o2], send_sem=ssem_o.at[0, d],
                recv_sem=rsem_o.at[0, o2], device_id=peer, device_id_type=MESH),
            pltpu.make_async_remote_copy(
                src_ref=mix.at[0], dst_ref=mix_all.at[o2], send_sem=ssem_o.at[1, d],
                recv_sem=rsem_o.at[1, o2], device_id=peer, device_id_type=MESH),
        ]

    for d in range(1, no):
        for copy in small(d, o):
            copy.start()
    for d in range(1, no):
        for copy in small(d, (o + d) % no):
            copy.wait_recv()
    for copy in local:
        copy.wait()
    table = pltpu.make_async_copy(own_all, own_tab, lsem.at[4])
    table.start()
    table.wait()

    def scan_source(s, carry):
        nxt[s, td] = td

        def back(n, following):
            t = td - 1 - n
            following = jnp.where(own_tab[s, 0, t] == o, t, following)
            nxt[s, t] = following
            return following

        lax.fori_loop(0, td, back, jnp.int32(td))
        return carry

    lax.fori_loop(0, no, scan_source, 0)

    def tile_piece(o2, i, send_sem, device):
        window = pl.ds(i * chunk_tiles, chunk_tiles)
        return pltpu.make_async_remote_copy(
            src_ref=tiles.at[o2, window], dst_ref=tiles.at[o2, window], send_sem=send_sem,
            recv_sem=rsem_t.at[o2, i], device_id=device, device_id_type=MESH,
        )

    def group_of(d):
        return ((g + d) % ng) * 2

    def hand_on(i):
        for d in range(1, ng):
            o2 = group_of(d) + c
            tile_piece(o2, i, ssem_c.at[d], partner).wait_recv()
            tile_piece(o2, i, ssem_c.at[d], partner).start()

    def compute(i):
        first = pl.multiple_of(i * cr, cr)
        total = jnp.zeros((cr, cols), jnp.float32)
        for slot in range(nv):
            block = gath[slot, pl.ds(first, cr), :]
            column = slot * kw + lax.broadcasted_iota(jnp.int32, (1, kw), 1)
            low, high = slot * kw // k_tile, ((slot + 1) * kw - 1) // k_tile
            parts = []
            for n in range(chunk_tiles):
                t = i * chunk_tiles + n
                flag = jnp.full((1, kw), amp_mask[low, t].astype(jnp.float32))
                for s in range(low + 1, high + 1):
                    flag = jnp.where(column >= s * k_tile, amp_mask[s, t].astype(jnp.float32), flag)
                flag = jnp.broadcast_to(flag, (tr, kw)).astype(jnp.bfloat16)
                parts.append(block[n * tr:(n + 1) * tr] * flag)
            total += jnp.dot(
                jnp.concatenate(parts, axis=0), ints_v[slot * kw:(slot + 1) * kw, :],
                preferred_element_type=jnp.float32,
            )
        ladder = total.astype(jnp.bfloat16)
        occ_col = jnp.transpose(jnp.broadcast_to(occ[i], (128, cr)))[:, :1]
        for n in range(chunk_tiles):
            t = i * chunk_tiles + n
            kept = ladder[n * tr:(n + 1) * tr] * keep[0, t].astype(jnp.float32).astype(jnp.bfloat16)
            mixed = jnp.dot(mix_all[own_s[0, t]], kept, preferred_element_type=jnp.float32)
            denominator = vir[...] - occ_col[n * tr:(n + 1) * tr]
            tiles[o, t] = (mixed / denominator).astype(jnp.bfloat16)

    def step(i, carry):
        @pl.when(i + ahead < nc)
        def _():
            spread(amps, v, i + ahead, True, True)

        for j in range(1, nz):
            @pl.when(z >= j)
            def _():
                slot = (z - j) * 2 + y
                arrive(slot, i)
                spread(gath.at[slot], slot, i, True, False)

            @pl.when(z + j < nz)
            def _():
                slot = (z + j) * 2 + y
                arrive(slot, i)
                spread(gath.at[slot], slot, i, False, True)

        for zz in range(nz):
            arrive(zz * 2 + (1 - y), i)
        compute(i)
        for d in range(1, ng):
            tile_piece(o, i, ssem_t.at[d], {"occ": group_of(d) + c, "vir": v}).start()
        tile_piece(o, i, ssem_c.at[0], partner).start()

        @pl.when(i > 0)
        def _():
            hand_on(i - 1)

        return carry

    lax.fori_loop(0, nc, step, 0)
    hand_on(nc - 1)

    def last(i, carry):
        for d in range(ng):
            tile_piece(group_of(d) + (1 - c), i, ssem_c.at[d], partner).wait_recv()
        return carry

    lax.fori_loop(0, nc, last, 0)

    def source(s, carry):
        def slot(k, position):
            t = nxt[s, position]
            tile = tiles[s, jnp.minimum(t, td - 1)]
            out[s * cap + k] = jnp.where(t < td, tile, jnp.zeros_like(tile))
            return jnp.minimum(t + 1, td)

        lax.fori_loop(0, cap, slot, jnp.int32(0))
        return carry

    lax.fori_loop(0, no, source, 0)

    def sent(whole, send_sem, recv_sem, device):
        pltpu.make_async_remote_copy(
            src_ref=whole, dst_ref=whole, send_sem=send_sem, recv_sem=recv_sem,
            device_id=device, device_id_type=MESH).wait_send()

    for zz in range(nz):
        @pl.when((z < nz - 1) & (zz <= z))
        def _():
            sent(gath.at[zz], ssem_g.at[0, zz], rsem_g.at[0, 0], side)

        @pl.when((z > 0) & (zz >= z))
        def _():
            sent(gath.at[zz], ssem_g.at[1, zz], rsem_g.at[0, 0], side)

        sent(gath.at[zz], ssem_g.at[2, zz], rsem_g.at[0, 0], side)
    for d in range(ng):
        sent(tiles.at[d], ssem_c.at[d], rsem_t.at[0, 0], partner)
        if d:
            sent(tiles.at[d], ssem_t.at[d], rsem_t.at[0, 0], partner)
    for d in range(1, no):
        for copy in small(d, o):
            copy.wait_send()


def shards(no, nv, amps, ints, amp_mask, keep_mask, owners, occ_energy, vir_energy, mix):
    td, k_tiles = amp_mask.shape
    rows, kw = amps.shape
    tr = rows // td
    cols = ints.shape[1]
    k_tile = ints.shape[0] // k_tiles
    cap = max(2, 2 * td // no)
    chunk_tiles = max(1, min(td, 128 // tr))
    nc = td // chunk_tiles
    cfg = (no, nv, td, tr, chunk_tiles, 2, k_tile)
    smem = pl.BlockSpec(memory_space=pltpu.SMEM)
    vmem = pl.BlockSpec(memory_space=pltpu.VMEM)
    hbm = pl.BlockSpec(memory_space=pl.ANY)
    ng, nz = no // 2, nv // 2
    own = owners.reshape(1, td)
    return pl.pallas_call(
        functools.partial(ladder_kernel, cfg),
        out_shape=jax.ShapeDtypeStruct((no * cap, tr, cols), jnp.bfloat16),
        in_specs=[hbm, hbm, smem, smem, smem, vmem, vmem, vmem, vmem],
        out_specs=vmem,
        scratch_shapes=[
            pltpu.VMEM((nv, rows, kw), jnp.bfloat16),
            pltpu.VMEM(ints.shape, jnp.bfloat16),
            pltpu.VMEM((no, td, tr, cols), jnp.bfloat16),
            pltpu.VMEM((no, tr, tr), jnp.bfloat16),
            pltpu.VMEM((no, 1, td), jnp.int32),
            pltpu.SMEM((no, 1, td), jnp.int32),
            pltpu.SMEM((no, td + 1), jnp.int32),
            pltpu.SemaphoreType.DMA((5,)),
            pltpu.SemaphoreType.DMA((nv, nc)),
            pltpu.SemaphoreType.DMA((3, nz)),
            pltpu.SemaphoreType.DMA((no, nc)),
            pltpu.SemaphoreType.DMA((ng,)),
            pltpu.SemaphoreType.DMA((ng,)),
            pltpu.SemaphoreType.DMA((2, no)),
            pltpu.SemaphoreType.DMA((2, no)),
        ],
        compiler_params=pltpu.CompilerParams(
            collective_id=0, has_side_effects=True, vmem_limit_bytes=60 * 1024 * 1024
        ),
    )(
        amps, ints, amp_mask.T, keep_mask.reshape(1, td), own, own,
        occ_energy.astype(jnp.float32).reshape(nc, 1, chunk_tiles * tr),
        vir_energy.reshape(1, cols), mix,
    )


def solution(mesh):
    in_specs = (
        P("occ", "vir"),
        P(None, "vir"),
        P("occ", None),
        P("occ", "vir"),
        P("occ", None),
        P("occ"),
        P("vir"),
        P("occ", None, None),
    )
    body = functools.partial(shards, mesh.shape["occ"], mesh.shape["vir"])
    return jax.shard_map(
        body, mesh=mesh, in_specs=in_specs, out_specs=P("occ", None, "vir"), check_vma=False
    )
```

```python
import functools

import jax
import jax.numpy as jnp
from jax import lax
from jax.experimental import pallas as pl
from jax.experimental.pallas import tpu as pltpu
from jax.sharding import PartitionSpec as P

MESH = pl.DeviceIdType.MESH


def ladder_kernel(
    cfg, amps, ints, amp_mask, keep, own_s, own_v, occ, vir, mix, out,
    gath, ints_v, occ_col, tiles, mix_all, own_all, own_tab, nxt,
    lsem, rsem_g, ssem_g, rsem_t, ssem_c, ssem_t, rsem_o, ssem_o,
):
    no, nv, td, tr, chunk_tiles, k_tile, ahead, ahead_side, stagger, lag, side_every = cfg
    ng, nz = no // 2, nv // 2
    rows, kw = amps.shape
    cols = ints.shape[1]
    cr = chunk_tiles * tr
    nc = rows // cr
    cap = out.shape[0] // no
    o, v = lax.axis_index("occ"), lax.axis_index("vir")
    g, c = o // 2, o % 2
    z, y = v // 2, v % 2
    partner = {"occ": g * 2 + (1 - c), "vir": v}
    side = {"occ": o, "vir": z * 2 + (1 - y)}
    above = {"occ": o, "vir": (z + 1) * 2 + y}
    below = {"occ": o, "vir": (z - 1) * 2 + y}

    local = [
        pltpu.make_async_copy(own_v, own_all.at[o], lsem.at[0]),
        pltpu.make_async_copy(ints, ints_v, lsem.at[3]),
        pltpu.make_async_copy(mix.at[0], mix_all.at[o], lsem.at[1]),
    ]
    for copy in local:
        copy.start()

    barrier = pltpu.get_barrier_semaphore()

    def greet(device):
        pl.semaphore_signal(barrier, inc=1, device_id=device, device_id_type=MESH)

    for d in range(1, no):
        greet({"occ": (o + d) % no, "vir": v})
    greet(side)

    @pl.when(z < nz - 1)
    def _():
        greet(above)

    @pl.when(z > 0)
    def _():
        greet(below)

    inner = jnp.where(z < nz - 1, 1, 0) + jnp.where(z > 0, 1, 0)
    pl.semaphore_wait(barrier, no + inner)

    def piece(src, slot, i, send_sem, device):
        window = pl.ds(pl.multiple_of(i * cr, cr), cr)
        return pltpu.make_async_remote_copy(
            src_ref=src.at[window], dst_ref=gath.at[slot, window], send_sem=send_sem,
            recv_sem=rsem_g.at[slot, i], device_id=device, device_id_type=MESH,
        )

    def side_first(i):
        return i % side_every == side_every // 2

    def spread(src, slot, i, up, down, across):
        if up:
            @pl.when(z < nz - 1)
            def _():
                piece(src, slot, i, ssem_g.at[0, slot], above).start()
        if down:
            @pl.when(z > 0)
            def _():
                piece(src, slot, i, ssem_g.at[1, slot], below).start()
        if across:
            piece(src, slot, i, ssem_g.at[2, slot], side).start()

    def arrive(slot, i):
        piece(gath.at[slot], slot, i, ssem_g.at[2, 0], side).wait_recv()

    for i in range(min(ahead_side, nc)):
        if i < ahead:
            spread(amps, v, i, True, True, False)
        spread(amps, v, i, False, False, True)

    def small(d, o2):
        peer = {"occ": (o + d) % no, "vir": v}
        return [
            pltpu.make_async_remote_copy(
                src_ref=own_v, dst_ref=own_all.at[o2], send_sem=ssem_o.at[0, d],
                recv_sem=rsem_o.at[0, o2], device_id=peer, device_id_type=MESH),
            pltpu.make_async_remote_copy(
                src_ref=mix.at[0], dst_ref=mix_all.at[o2], send_sem=ssem_o.at[1, d],
                recv_sem=rsem_o.at[1, o2], device_id=peer, device_id_type=MESH),
        ]

    for d in range(1, no):
        for copy in small(d, o):
            copy.start()

    def prepare():
        for d in range(1, no):
            for copy in small(d, (o + d) % no):
                copy.wait_recv()
        for copy in local:
            copy.wait()
        table = pltpu.make_async_copy(own_all, own_tab, lsem.at[2])
        table.start()
        table.wait()

        def scan_source(s, carry):
            nxt[s, td] = td

            def back(n, following):
                t = td - 1 - n
                following = jnp.where(own_tab[s, 0, t] == o, t, following)
                nxt[s, t] = following
                return following

            lax.fori_loop(0, td, back, jnp.int32(td))
            return carry

        lax.fori_loop(0, no, scan_source, 0)

    gath[v] = amps[...]
    lanes = occ.shape[1]
    for r in range(occ.shape[0]):
        row = jnp.broadcast_to(occ[...].astype(jnp.float32)[r:r + 1], (128, lanes))
        occ_col[r * lanes:(r + 1) * lanes, :] = jnp.transpose(row)

    def tile_piece(o2, i, send_sem, device):
        window = pl.ds(i * chunk_tiles, chunk_tiles)
        return pltpu.make_async_remote_copy(
            src_ref=tiles.at[o2, window], dst_ref=tiles.at[o2, window], send_sem=send_sem,
            recv_sem=rsem_t.at[o2, i], device_id=device, device_id_type=MESH,
        )

    def group_of(d):
        return ((g + d) % ng) * 2

    def hand_on(i):
        for d in range(1, ng):
            o2 = group_of(d) + c
            tile_piece(o2, i, ssem_c.at[d], partner).wait_recv()
            tile_piece(o2, i, ssem_c.at[d], partner).start()

    def compute(i):
        first = pl.multiple_of(i * cr, cr)
        total = jnp.zeros((cr, cols), jnp.float32)
        for slot in range(nv):
            block = gath[slot, pl.ds(first, cr), :]
            column = slot * kw + lax.broadcasted_iota(jnp.int32, (1, kw), 1)
            low, high = slot * kw // k_tile, ((slot + 1) * kw - 1) // k_tile
            parts = []
            for n in range(chunk_tiles):
                t = i * chunk_tiles + n
                flag = jnp.full((1, kw), amp_mask[low, t].astype(jnp.float32))
                for s in range(low + 1, high + 1):
                    flag = jnp.where(column >= s * k_tile, amp_mask[s, t].astype(jnp.float32), flag)
                flag = jnp.broadcast_to(flag, (tr, kw)).astype(jnp.bfloat16)
                parts.append(block[n * tr:(n + 1) * tr] * flag)
            total += jnp.dot(
                jnp.concatenate(parts, axis=0), ints_v[slot * kw:(slot + 1) * kw, :],
                preferred_element_type=jnp.float32,
            )
        ladder = total.astype(jnp.bfloat16)
        for n in range(chunk_tiles):
            t = i * chunk_tiles + n
            kept = ladder[n * tr:(n + 1) * tr] * keep[0, t].astype(jnp.float32).astype(jnp.bfloat16)
            mixed = jnp.dot(mix_all[own_s[0, t]], kept, preferred_element_type=jnp.float32)
            energy = occ_col[pl.ds(pl.multiple_of(t * tr, tr), tr), :]
            denominator = vir[...] - jnp.concatenate([energy] * (cols // 128), axis=1)
            tiles[o, t] = (mixed / denominator).astype(jnp.bfloat16)

    def within(i, body):
        @pl.when((i >= 0) & (i < nc))
        def _():
            body(i)

    def send_own(i):
        spread(amps, v, i, True, True, False)

    def send_side(i):
        spread(amps, v, i, False, False, True)

    def turn(i):
        @pl.when(side_first(i))
        def _():
            slot = z * 2 + (1 - y)
            arrive(slot, i)
            spread(gath.at[slot], slot, i, True, True, False)

    def forward(j, i):
        for step_z, up in ((-j, True), (j, False)):
            near = z + step_z

            @pl.when((near >= 0) & (near < nz))
            def _():
                slot = near * 2 + y
                other = near * 2 + (1 - y)
                arrive(slot, i)
                spread(gath.at[slot], slot, i, up, not up, False)

                @pl.when(side_first(i))
                def _():
                    arrive(other, i)
                    spread(gath.at[other], other, i, up, not up, False)

                @pl.when(jnp.logical_not(side_first(i)))
                def _():
                    spread(gath.at[slot], slot, i, False, False, True)

    def finish(i):
        @pl.when(i == 0)
        def _():
            prepare()

        @pl.when(jnp.logical_not(side_first(i)))
        def _():
            for zz in range(nz):
                arrive(zz * 2 + (1 - y), i)

        compute(i)
        for d in range(1, ng):
            tile_piece(o, i, ssem_t.at[d], {"occ": group_of(d) + c, "vir": v}).start()
        tile_piece(o, i, ssem_c.at[0], partner).start()

    def step(s, carry):
        within(s + ahead, send_own)
        within(s + ahead_side, send_side)
        within(s, turn)
        for j in range(1, nz):
            within(s - stagger * j, functools.partial(forward, j))
        within(s - lag, finish)
        within(s - lag - 1, hand_on)
        return carry

    lax.fori_loop(0, nc + lag + 1, step, 0)

    def last(i, carry):
        for d in range(ng):
            tile_piece(group_of(d) + (1 - c), i, ssem_c.at[d], partner).wait_recv()
        return carry

    lax.fori_loop(0, nc, last, 0)

    def source(s, carry):
        def slot(k, position):
            t = nxt[s, position]
            tile = tiles[s, jnp.minimum(t, td - 1)]
            out[s * cap + k] = jnp.where(t < td, tile, jnp.zeros_like(tile))
            return jnp.minimum(t + 1, td)

        lax.fori_loop(0, cap, slot, jnp.int32(0))
        return carry

    lax.fori_loop(0, no, source, 0)

    def sent(whole, send_sem, recv_sem, device):
        pltpu.make_async_remote_copy(
            src_ref=whole, dst_ref=whole, send_sem=send_sem, recv_sem=recv_sem,
            device_id=device, device_id_type=MESH).wait_send()

    turned = sum(1 for i in range(nc) if side_first(i)) * cr
    full = gath.shape[1]
    for zz in range(nz):
        for slot, count in ((zz * 2 + y, full), (zz * 2 + (1 - y), turned)):
            if count:
                whole = gath.at[zz, pl.ds(0, count)]

                @pl.when((z < nz - 1) & (zz <= z))
                def _():
                    sent(whole, ssem_g.at[0, slot], rsem_g.at[0, 0], side)

                @pl.when((z > 0) & (zz >= z))
                def _():
                    sent(whole, ssem_g.at[1, slot], rsem_g.at[0, 0], side)

        @pl.when(zz == z)
        def _():
            sent(gath.at[zz], ssem_g.at[2, v], rsem_g.at[0, 0], side)

        if full > turned:
            @pl.when(zz != z)
            def _():
                part = gath.at[zz, pl.ds(0, full - turned)]
                sent(part, ssem_g.at[2, zz * 2 + y], rsem_g.at[0, 0], side)
    for d in range(ng):
        sent(tiles.at[d], ssem_c.at[d], rsem_t.at[0, 0], partner)
        if d:
            sent(tiles.at[d], ssem_t.at[d], rsem_t.at[0, 0], partner)
    for d in range(1, no):
        for copy in small(d, o):
            copy.wait_send()


def shards(no, nv, amps, ints, amp_mask, keep_mask, owners, occ_energy, vir_energy, mix):
    td, k_tiles = amp_mask.shape
    rows, kw = amps.shape
    tr = rows // td
    cols = ints.shape[1]
    k_tile = ints.shape[0] // k_tiles
    cap = max(2, 2 * td // no)
    chunk_tiles = max(1, min(td, 128 // tr))
    nc = td // chunk_tiles
    ahead, ahead_side, stagger, side_every = 2, 6, 1, 8
    lag = stagger * (nv // 2 - 1) + 1
    cfg = (no, nv, td, tr, chunk_tiles, k_tile, ahead, ahead_side, stagger, lag, side_every)
    smem = pl.BlockSpec(memory_space=pltpu.SMEM)
    vmem = pl.BlockSpec(memory_space=pltpu.VMEM)
    ng, nz = no // 2, nv // 2
    own = owners.reshape(1, td)
    return pl.pallas_call(
        functools.partial(ladder_kernel, cfg),
        out_shape=jax.ShapeDtypeStruct((no * cap, tr, cols), jnp.bfloat16),
        in_specs=[vmem, pl.BlockSpec(memory_space=pl.ANY), smem, smem, smem, vmem, vmem, vmem, vmem],
        out_specs=vmem,
        scratch_shapes=[
            pltpu.VMEM((nv, rows, kw), jnp.bfloat16),
            pltpu.VMEM(ints.shape, jnp.bfloat16),
            pltpu.VMEM((rows, 128), jnp.float32),
            pltpu.VMEM((no, td, tr, cols), jnp.bfloat16),
            pltpu.VMEM((no, tr, tr), jnp.bfloat16),
            pltpu.VMEM((no, 1, td), jnp.int32),
            pltpu.SMEM((no, 1, td), jnp.int32),
            pltpu.SMEM((no, td + 1), jnp.int32),
            pltpu.SemaphoreType.DMA((4,)),
            pltpu.SemaphoreType.DMA((nv, nc)),
            pltpu.SemaphoreType.DMA((3, nv)),
            pltpu.SemaphoreType.DMA((no, nc)),
            pltpu.SemaphoreType.DMA((ng,)),
            pltpu.SemaphoreType.DMA((ng,)),
            pltpu.SemaphoreType.DMA((2, no)),
            pltpu.SemaphoreType.DMA((2, no)),
        ],
        compiler_params=pltpu.CompilerParams(
            collective_id=0, has_side_effects=True, vmem_limit_bytes=60 * 1024 * 1024
        ),
    )(
        amps, ints, amp_mask.T, keep_mask.reshape(1, td), own, own,
        occ_energy.reshape(rows // 128, 128),
        vir_energy.reshape(1, cols), mix,
    )


def solution(mesh):
    in_specs = (
        P("occ", "vir"),
        P(None, "vir"),
        P("occ", None),
        P("occ", "vir"),
        P("occ", None),
        P("occ"),
        P("vir"),
        P("occ", None, None),
    )
    body = functools.partial(shards, mesh.shape["occ"], mesh.shape["vir"])
    return jax.shard_map(
        body, mesh=mesh, in_specs=in_specs, out_specs=P("occ", None, "vir"), check_vma=False
    )
```
